256 devices in a mesh: aux: 64 (over x, z, core), pair: 4 (over y).
Axes of the slice: x: 4, y: 4, z: 8, core: 2. Of those that a mesh axis runs over, the one named last changes fastest.
Arguments:
- shell_ints: bfloat16 [16384, 16, 64, 64], P('aux', 'pair'), may hold values from -0.119628906 to 0.119628906
- block_ids: int32 [16, 2], P('pair'), may hold values from 0 to 15
- block_count: int32 [4], P('pair'), may hold values from 1 to 4, 10 in all
- occ_coef: bfloat16 [16, 64, 512], replicated, may hold values from -0.75 to 0.75
- occ_pick: int32 [512], replicated, may hold values from 0 to 511, each once
- vir_coef: bfloat16 [16, 64, 384], replicated, may hold values from -0.1875 to 0.1875
- occ_energy: float32 [512], replicated, may hold values from -1.5 to -0.3
- vir_energy: float32 [384], replicated, may hold values from 0.2 to 3
Outputs:
- pair_energy: float32 [64], P('aux')
- vir_density: float32 [384, 384], P('pair')
The draws below stay inside these ranges and needn't reach their ends.
Inputs may be any that keep to these rules, and one draw needn't show every extreme that they name: `block_ids`: basis block numbers of the mu and nu side. `block_count`: the busiest group holds exactly 4 live blocks. `occ_pick`: each of the 512 numbers appears once.
All inputs are finite; a program needn't handle non-finite values.
Results may differ from the reference program's by a relative error of at most 0.01.
Values may be sent and summed in bfloat16 or wider, within the bound.
A program may use at most 128 MiB of HBM per device.

```python
import math
import jax
import jax.numpy as jnp
import numpy as np
from jax import lax

Q_DEV = 256
BF = 64
NB_DEV = 4
NAOB = 16
NOCC = 512
VB = 384
NAUX = 16384
NBLK = 16
NGROUP = 4
N_AUX = 64
N_PAIR = 4


def plant(entries, own_key, smallest, top_value):
    spot = [jax.random.randint(jax.random.fold_in(own_key, axis), (), 0, length) for axis, length in enumerate(entries.shape)]
    widest = entries.shape.index(max(entries.shape))
    next_to = spot[:widest] + [(spot[widest] + 1) % entries.shape[widest]] + spot[widest + 1:]
    return entries.at[tuple(spot)].set(smallest).at[tuple(next_to)].set(top_value)


def block_levels(rng, shape, cuts, low, top_value):
    loudness = 1.0
    for axis_at, blocks in cuts:
        steps = jax.random.uniform(jax.random.fold_in(jax.random.fold_in(rng, 6), axis_at), (blocks,), jnp.float32, low / len(cuts), top_value / len(cuts))
        loudness = loudness * jnp.repeat(jnp.exp(steps), shape[axis_at] // blocks).reshape((-1,) + (1,) * (len(shape) - 1 - axis_at))
    return loudness


def split_up(amount, total, bound, slope):
    portions = [(1 << 20) // math.isqrt(grade ** slope) + 1 for grade in range(2, amount + 1)]
    spare, counts = total - bound - (amount - 1), [1] * (amount - 1)
    while spare > 0:
        candidates = [i for i in range(amount - 1) if counts[i] < bound]
        mass, budget = sum([portions[i] for i in candidates]), spare
        for i in candidates:
            addition = min(bound - counts[i], max(1, budget * portions[i] // mass), spare)
            counts[i] = counts[i] + addition
            spare = spare - addition
    return np.array([bound] + counts)


def ragged_sizes(stream_key, amount, total, reach, skew):
    if amount == 2:
        one = jax.random.randint(stream_key, (), max(1, total - reach), min(reach, total - 1) + 1)
        return jnp.stack([one, total - one])
    tallies = jnp.asarray(split_up(amount, total, reach, skew), jnp.int32)
    pairs = (amount - 1) // 2
    source_of, receiver = tallies[1:1 + 2 * pairs:2], tallies[2:2 + 2 * pairs:2]
    margin = jnp.minimum(source_of - 1, reach - receiver)
    passed = jax.random.randint(jax.random.fold_in(stream_key, 1), (pairs,), 0, 1 << 20) % (margin + 1)
    tallies = tallies.at[1:1 + 2 * pairs:2].set(source_of - passed).at[2:2 + 2 * pairs:2].set(receiver + passed)
    return tallies[jax.random.permutation(jax.random.fold_in(stream_key, 2), amount)]


def normal_values(key, shape, spread, most, split=(), held_as=jnp.bfloat16):
    array = spread * jax.random.normal(key, shape, jnp.float32)
    if split:
        array = array * block_levels(key, shape, split, -0.22, 0.18)
    return jnp.clip(array, -most, most).astype(held_as)


def setup_inputs(seed: int = 0) -> dict:
    arg_keys = jax.random.split(jax.random.key(seed), 9)
    return {
        "shell_ints": normal_values(arg_keys[0], (NAUX, NBLK, BF, BF), 0.02, 0.119628906, ((0, 64), (1, 4))),
        "block_ids": plant(jax.random.randint(arg_keys[1], (NBLK, 2), 0, NAOB), jax.random.fold_in(arg_keys[1], 1), 0, NAOB - 1).astype(jnp.int32),
        "block_count": ragged_sizes(arg_keys[2], NGROUP, NB_DEV * NGROUP * 5 // 8, NB_DEV, 2).astype(jnp.int32),
        "occ_coef": normal_values(arg_keys[3], (NAOB, BF, NOCC), BF ** -0.5, 0.75),
        "occ_pick": jax.random.permutation(arg_keys[4], NOCC).astype(jnp.int32),
        "vir_coef": normal_values(arg_keys[5], (NAOB, BF, VB), (NBLK * BF) ** -0.5, 0.1875),
        "occ_energy": jnp.clip(jax.random.uniform(arg_keys[6], (NOCC,), jnp.float32, -1.5, -0.3), -1.5, -0.3),
        "vir_energy": jnp.clip(jax.random.uniform(arg_keys[7], (VB,), jnp.float32, 0.2, 3.0), 0.2, 3.0),
    }


def reference(shell_ints, block_ids, block_count, occ_coef, occ_pick, vir_coef, occ_energy, vir_energy):
    batch = occ_pick[:N_AUX]
    occ_rows = occ_coef[block_ids[:, 1]][:, :, batch]
    slot_index = jnp.arange(NBLK, dtype=jnp.int32) % NB_DEV
    group_index = jnp.arange(NBLK, dtype=jnp.int32) // NB_DEV
    live = (slot_index < block_count[group_index]).astype(jnp.bfloat16)
    vir_rows = vir_coef[block_ids[:, 0]] * live[:, None, None]
    vir_groups = vir_rows.reshape(N_PAIR, NB_DEV * BF, VB).astype(jnp.float32)
    shards = shell_ints.reshape(N_AUX, Q_DEV, NBLK, BF, BF)

    def one_shard(ints):
        half = jnp.einsum("qkmn,kni->qikm", ints.astype(jnp.float32), occ_rows.astype(jnp.float32)).astype(jnp.bfloat16)
        half = half.reshape(Q_DEV, N_AUX, N_PAIR, NB_DEV * BF).astype(jnp.float32)
        parts = jnp.einsum("qigk,gka->gqia", half, vir_groups)
        parts = lax.optimization_barrier(parts.astype(jnp.bfloat16)).astype(jnp.float32)
        return jnp.sum(parts, axis=0).astype(jnp.bfloat16)

    fitted = lax.map(one_shard, shards).reshape(NAUX, N_AUX, VB)
    levels = occ_energy[batch]
    partners = (jnp.arange(N_AUX, dtype=jnp.int32) - N_AUX // 2) % N_AUX

    def pair_terms(total, g):
        h = partners[g]
        left = lax.dynamic_index_in_dim(fitted, g, 1, keepdims=False)
        right = lax.dynamic_index_in_dim(fitted, h, 1, keepdims=False)
        coulomb = jnp.dot(left.T, right, preferred_element_type=jnp.float32)
        denom = levels[g] + levels[h] - vir_energy[:, None] - vir_energy[None, :]
        amplitude = coulomb / denom
        energy = jnp.sum(amplitude * (2.0 * coulomb - coulomb.T))
        density = jnp.dot(2.0 * amplitude - amplitude.T, amplitude.T, precision=lax.Precision.HIGHEST)
        return total + density, energy

    vir_density, pair_energy = lax.scan(pair_terms, jnp.zeros((VB, VB), jnp.float32), jnp.arange(N_AUX, dtype=jnp.int32))
    return pair_energy, vir_density
```

```python
import functools

import jax
import jax.numpy as jnp
from jax import lax
from jax.experimental import pallas as pl
from jax.experimental.pallas import tpu as pltpu
from jax.sharding import PartitionSpec as P

F32, BF16, I32 = jnp.float32, jnp.bfloat16, jnp.int32
MESH = pl.DeviceIdType.MESH
NX, NY, NZ, NC = 4, 4, 8, 2
NT = (((1,), (1,)), ((), ()))
DMA = pltpu.SemaphoreType.DMA


def dot(a, b, dims=(((1,), (0,)), ((), ()))):
    return lax.dot_general(a, b, dims, preferred_element_type=F32)


def onehot(mask):
    return jnp.where(mask, 1.0, 0.0).astype(BF16)


def iota(shape, axis):
    return lax.broadcasted_iota(I32, shape, axis)


def kernel(
    ids, count, pick_s, eocc,
    ints_hbm, occ, pick_v, vir, evir,
    out_d, out_e,
    ints, lhs, half, vir_t, vt, meta, meta_in,
    far, near, relay, part,
    cbuf, core_in, x_in, zsum, z_in, call, amp, amp_t, mix,
    dblk, d_in, dy, p2_in, p3, fin,
    ints_sem, meta_ss, meta_rs, far_ss, far_rs, near_ss, near_rs, part_ss, part_rs,
    core_ss, core_rs, x_ss, x_rs, z_ss, z_rs, ag_ss, ag_rs, y_ss, y_rs,
    p2_ss, p2_rs, p3_ss, p3_rs, f_ss, f_rs,
):
    a = lax.axis_index("aux")
    p = lax.axis_index("pair")
    c = lax.rem(a, NC)
    z = lax.rem(lax.div(a, NC), NZ)
    x = lax.div(a, NC * NZ)

    def dev(px, py, pz, pc):
        return {"aux": (px * NZ + pz) * NC + pc, "pair": py}

    def remote(src, dst, ss, rs, to):
        return pltpu.make_async_remote_copy(
            src_ref=src, dst_ref=dst, send_sem=ss, recv_sem=rs, device_id=to, device_id_type=MESH
        )

    def ypeer(step):
        return dev(x, lax.rem(p + step + NY, NY), z, c)

    loads = [pltpu.make_async_copy(ints_hbm.at[s], ints.at[s], ints_sem.at[s]) for s in range(4)]
    for load in loads:
        load.start()

    barrier = pltpu.get_barrier_semaphore()

    def greet(to):
        pl.semaphore_signal(barrier, inc=1, device_id=to, device_id_type=MESH)

    for step in range(1, NY):
        greet(ypeer(step))

    def greet_xc(o, carry):
        s = lax.rem(x * NC + c + o, NX * NC)
        greet(dev(lax.div(s, NC), p, z, lax.rem(s, NC)))
        return carry

    lax.fori_loop(1, NX * NC, greet_xc, 0)

    def greet_z(o, carry):
        pz = lax.rem(z + o, NZ)
        greet(dev(x, p, pz, 0))
        greet(dev(x, p, pz, 1))
        return carry

    lax.fori_loop(1, NZ, greet_z, 0)

    lane = iota((8, 256), 1)
    slot = lax.shift_right_logical(lane, 6)
    mine = jnp.full((8, 256), ids[0, 0], I32)
    for k in range(1, 4):
        mine = jnp.where(slot == k, ids[k, 0], mine)
    meta[...] = jnp.where(slot < count[0], mine * 64 + (lane & 63), -1)

    pick_t = onehot(iota((512, 64), 0) == pick_v[:, 0:64])
    r = iota((512, 64), 0)
    orbital = (lax.shift_right_logical(r, 3) & 1) * 32 + (lax.shift_right_logical(r, 4) & 3) * 8
    orbital = orbital + lax.shift_right_logical(r, 6)
    pick_e = dot(onehot(iota((512, 64), 1) == orbital), pick_t, NT).astype(BF16)
    same = (iota((512, 512), 0) & 7) == lax.shift_right_logical(iota((512, 512), 1), 6)

    def make_lhs(s, carry):
        rows = occ[ids[s, 1]]
        tiled = jnp.concatenate([rows] * 8, axis=0)
        lhs[s] = jnp.where(same, dot(pick_e, tiled, NT), 0.0).astype(BF16)
        return carry

    lax.fori_loop(0, 4, make_lhs, 0)

    pl.semaphore_wait(barrier, 3 + 7 + 14)

    metas = [
        remote(meta, meta_in.at[0], meta_ss.at[0], meta_rs.at[0], ypeer(-1)),
        remote(meta, meta_in.at[1], meta_ss.at[1], meta_rs.at[1], ypeer(1)),
    ]
    for m in metas:
        m.start()
    for load in loads:
        load.wait()

    def far_copy(j, d):
        t = lax.rem(p + 2, NY)
        return remote(half.at[pl.ds(j * 8 + t * 2, 2)], far.at[j], far_ss.at[j], far_rs.at[j], ypeer(d))

    def near_copy(j, d):
        t = lax.rem(p - d + NY, NY)
        return remote(half.at[pl.ds(j * 8 + t * 2, 2)], near.at[j], near_ss.at[j], near_rs.at[j], ypeer(-d))

    def part_copy(j, d):
        return remote(relay.at[j], part.at[j], part_ss.at[j], part_rs.at[j], ypeer(d))

    def half_pass(q, carry):
        def one_slot(s, inner):
            rows = lhs[s, pl.ds(pl.multiple_of(q * 128, 128), 128), :]
            for h in range(4):
                u = dot(rows, ints[s, 2 * h]).reshape(16, 8, 256)
                v = dot(rows, ints[s, 2 * h + 1]).reshape(16, 8, 256)
                block = jnp.concatenate([u, v], axis=1).astype(BF16)
                half[pl.ds(q * 16, 16), pl.ds(pl.multiple_of(s * 64 + h * 16, 16), 16), :] = block
            return inner

        lax.fori_loop(0, 4, one_slot, 0)
        far_copy(2 * q, 1).start()
        far_copy(2 * q + 1, -1).start()
        near_copy(2 * q, 1).start()
        near_copy(2 * q + 1, -1).start()
        return carry

    lax.fori_loop(0, 4, half_pass, 0)

    vir_t[...] = vir[...].astype(F32).T.astype(BF16)
    row = iota((1024, 256), 0)
    vt[0] = dot(vir_t[...], onehot(row == meta[0:1, :])).astype(BF16)
    for g in range(2):
        metas[g].wait_recv()
        vt[1 + g] = dot(vir_t[...], onehot(row == meta_in[g, 0:1, :])).astype(BF16)

    def do_relay(j, d):
        far_copy(j, d).wait_recv()
        t = lax.rem(p + d + NY, NY)
        for gh in range(2):
            total = dot(vt[2 if d == 1 else 1], far[j, gh]) + dot(vt[0], half[j * 8 + t * 2 + gh])
            relay[j, gh] = total.astype(BF16)
        part_copy(j, d).start()

    def relay_pass(q, carry):
        do_relay(2 * q, 1)
        do_relay(2 * q + 1, -1)
        return carry

    lax.fori_loop(0, 4, relay_pass, 0)

    def core_copy(j):
        return remote(cbuf.at[j, 1 - c], core_in.at[j], core_ss.at[j], core_rs.at[j], dev(x, p, z, 1 - c))

    def x_copy(j, o):
        q = lax.rem(x + o, NX)
        return remote(
            core_in.at[j, q], x_in.at[j, o - 1], x_ss.at[j, o - 1], x_rs.at[j, o - 1], dev(q, p, z, c)
        )

    def z_copy(j, o):
        return remote(zsum.at[j], z_in.at[o - 1], z_ss.at[j], z_rs.at[o - 1], dev(x, p, j, c))

    def do_target(j, d):
        near_copy(j, d).wait_recv()
        part_copy(j, d).wait_recv()
        fitted = []
        for gh in range(2):
            total = part[j, gh].astype(F32) + dot(vt[1 if d == 1 else 2], near[j, gh])
            total = total + dot(vt[0], half[j * 8 + p * 2 + gh])
            fitted.append(total.astype(BF16))
        block = dot(fitted[0], fitted[1], NT)
        for q in range(4):
            for pc in range(2):
                lo = q * 96 + pc * 48
                cbuf[j, pc, q] = block[lo : lo + 48]
        core_copy(j).start()

    def do_core(j):
        core_copy(j).wait_recv()
        core_in[j] = core_in[j] + cbuf[j, c]
        for o in range(1, NX):
            x_copy(j, o).start()

    def do_x(j):
        total = core_in[j, x]
        for o in range(1, NX):
            x_copy(j, o).wait_recv()
            total = total + x_in[j, o - 1]
        zsum[j] = total

        @pl.when(z != j)
        def _():
            z_copy(j, lax.rem(z - j + NZ, NZ)).start()

    def target_pass(q, carry):
        do_target(2 * q, 1)

        @pl.when(q > 0)
        def _():
            do_core(2 * q - 1)
            do_x(2 * q - 2)

        do_target(2 * q + 1, -1)
        do_core(2 * q)

        @pl.when(q > 0)
        def _():
            do_x(2 * q - 1)

        return carry

    lax.fori_loop(0, 4, target_pass, 0)
    do_core(7)
    do_x(6)
    do_x(7)

    total = zsum[z]
    for o in range(1, NZ):
        z_copy(z, o).wait_recv()
        total = total + z_in[o - 1]
    slab = x * NC + c
    call[slab] = total

    def ag_copy(o, src):
        s = lax.rem(slab + o, NX * NC)
        to = dev(lax.div(s, NC), p, z, lax.rem(s, NC))
        return remote(call.at[src], call.at[src], ag_ss.at[o - 1], ag_rs.at[src], to)

    for o in range(1, NX * NC):
        ag_copy(o, slab).start()
    for o in range(1, NX * NC):
        ag_copy(o, lax.rem(slab + o, NX * NC)).wait_recv()

    k = p * NZ + z
    level = eocc[pick_s[k]] + eocc[pick_s[k + 32]]
    block = call[...].reshape(384, 384)
    block_t = block.T
    across = jnp.broadcast_to(evir[...], (384, 384))
    denom = level - across.T - across
    amplitude = block / denom
    energy = jnp.sum(amplitude * (2.0 * block - block_t))
    amplitude_t = block_t / denom
    first = c == 0
    amp[...] = jnp.where(first, amplitude, amplitude_t)
    mix[...] = jnp.where(first, 2.0 * amplitude - amplitude_t, 2.0 * amplitude_t - amplitude)
    rows = jnp.concatenate([mix[pl.ds(pl.multiple_of(y * 96 + x * 24, 8), 24), :] for y in range(4)], axis=0)
    share = lax.dot_general(rows, amp[...], NT, precision=lax.Precision.HIGHEST, preferred_element_type=F32)
    tip = jnp.where((iota((8, 384), 1) == k) & first, energy, 0.0)
    for y in range(4):
        dblk[y, 0:24, :] = share[y * 24 : y * 24 + 24]
        dblk[y, 24:32, :] = tip

    def y_copy(o):
        y = lax.rem(p + o, NY)
        return remote(dblk.at[y], d_in.at[o - 1], y_ss.at[o - 1], y_rs.at[o - 1], dev(x, y, z, c))

    for o in range(1, NY):
        y_copy(o).start()
    total = dblk[p]
    for o in range(1, NY):
        y_copy(o).wait_recv()
        total = total + d_in[o - 1]
    dy[...] = total.reshape(4, 8, 384)

    line = z * NC + c

    def p2_copy(t, src):
        return remote(dy.at[t], p2_in.at[src], p2_ss.at[t], p2_rs.at[src], dev(x, p, 2 * t, 0))

    for t in range(4):

        @pl.when(line != 4 * t)
        def _():
            p2_copy(t, line).start()

    root = lax.rem(line, 4) == 0
    mytile = lax.div(line, 4)

    def p3_copy(o, src):
        return remote(p3.at[src], p3.at[src], p3_ss.at[o - 1], p3_rs.at[src], dev(lax.rem(x + o, NX), p, z, c))

    def f_copy(o, tile):
        to = lax.rem(line + o, NZ * NC)
        return remote(fin.at[tile], fin.at[tile], f_ss.at[o - 1], f_rs.at[tile], dev(x, p, lax.div(to, NC), lax.rem(to, NC)))

    @pl.when(root)
    def _():
        p2_in[line] = dy[mytile]

        def arrive(o, carry):
            p2_copy(0, lax.rem(line + o, NZ * NC)).wait_recv()
            return carry

        lax.fori_loop(1, NZ * NC, arrive, 0)
        p3[x] = jnp.sum(p2_in[...], axis=0)
        for o in range(1, NX):
            p3_copy(o, x).start()
        for o in range(1, NX):
            p3_copy(o, lax.rem(x + o, NX)).wait_recv()
        fin[mytile] = p3[...]

        def send(o, carry):
            f_copy(o, mytile).start()
            return carry

        lax.fori_loop(1, NZ * NC, send, 0)

    for t in range(4):

        @pl.when(line != 4 * t)
        def _():
            f_copy(1, t).wait_recv()

    for q in range(4):
        for t in range(3):
            out_d[q * 24 + t * 8 : q * 24 + t * 8 + 8, :] = fin[t, q]
    mine_e = fin[3, 0][0:1, :]
    out_e[0] = jnp.sum(jnp.where(iota((1, 384), 1) == lax.rem(a, 32), mine_e, 0.0))

    for m in metas:
        m.wait_send()

    def sent(q, carry):
        for j, d in ((2 * q, 1), (2 * q + 1, -1)):
            far_copy(j, d).wait_send()
            near_copy(j, d).wait_send()
            part_copy(j, d).wait_send()
            core_copy(j).wait_send()
            for o in range(1, NX):
                x_copy(j, o).wait_send()

            @pl.when(z != j)
            def _():
                z_copy(j, 1).wait_send()

        return carry

    lax.fori_loop(0, 4, sent, 0)
    for o in range(1, NX * NC):
        ag_copy(o, slab).wait_send()
    for o in range(1, NY):
        y_copy(o).wait_send()
    for t in range(4):

        @pl.when(line != 4 * t)
        def _():
            p2_copy(t, line).wait_send()

    @pl.when(root)
    def _():
        for o in range(1, NX):
            p3_copy(o, x).wait_send()

        def done(o, carry):
            f_copy(o, mytile).wait_send()
            return carry

        lax.fori_loop(1, NZ * NC, done, 0)


def per_device(
    shell_ints, block_ids, block_count, occ_coef, occ_pick, vir_coef, occ_energy, vir_energy
):
    ints = jnp.transpose(shell_ints, (1, 2, 3, 0)).reshape(4, 8, 512, 256)
    smem = pl.BlockSpec(memory_space=pltpu.SMEM)
    vmem = pl.BlockSpec(memory_space=pltpu.VMEM)
    density, energy = pl.pallas_call(
        kernel,
        out_shape=(jax.ShapeDtypeStruct((96, 384), F32), jax.ShapeDtypeStruct((1,), F32)),
        in_specs=[smem] * 4 + [pl.BlockSpec(memory_space=pl.ANY)] + [vmem] * 4,
        out_specs=(vmem, smem),
        scratch_shapes=[
            pltpu.VMEM((4, 8, 512, 256), BF16),
            pltpu.VMEM((4, 512, 512), BF16),
            pltpu.VMEM((64, 256, 256), BF16),
            pltpu.VMEM((384, 1024), BF16),
            pltpu.VMEM((3, 384, 256), BF16),
            pltpu.VMEM((8, 256), I32),
            pltpu.VMEM((2, 8, 256), I32),
            pltpu.VMEM((8, 2, 256, 256), BF16),
            pltpu.VMEM((8, 2, 256, 256), BF16),
            pltpu.VMEM((8, 2, 384, 256), BF16),
            pltpu.VMEM((8, 2, 384, 256), BF16),
            pltpu.VMEM((8, 2, 4, 48, 384), F32),
            pltpu.VMEM((8, 4, 48, 384), F32),
            pltpu.VMEM((8, 3, 48, 384), F32),
            pltpu.VMEM((8, 48, 384), F32),
            pltpu.VMEM((7, 48, 384), F32),
            pltpu.VMEM((8, 48, 384), F32),
            pltpu.VMEM((384, 384), F32),
            pltpu.VMEM((8, 128), F32),
            pltpu.VMEM((384, 384), F32),
            pltpu.VMEM((4, 32, 384), F32),
            pltpu.VMEM((3, 32, 384), F32),
            pltpu.VMEM((4, 8, 384), F32),
            pltpu.VMEM((16, 8, 384), F32),
            pltpu.VMEM((4, 8, 384), F32),
            pltpu.VMEM((4, 4, 8, 384), F32),
            DMA((4,)),
            DMA((2,)), DMA((2,)),
            DMA((8,)), DMA((8,)),
            DMA((8,)), DMA((8,)),
            DMA((8,)), DMA((8,)),
            DMA((8,)), DMA((8,)),
            DMA((8, 3)), DMA((8, 3)),
            DMA((8,)), DMA((7,)),
            DMA((7,)), DMA((8,)),
            DMA((3,)), DMA((3,)),
            DMA((4,)), DMA((16,)),
            DMA((3,)), DMA((4,)),
            DMA((15,)), DMA((4,)),
        ],
        compiler_params=pltpu.CompilerParams(
            collective_id=0, has_side_effects=True, vmem_limit_bytes=56 << 20
        ),
    )(
        block_ids, block_count, occ_pick, occ_energy,
        ints, occ_coef, occ_pick.reshape(1, 512), vir_coef.reshape(1024, 384),
        vir_energy.reshape(1, 384),
    )
    return (energy, density)


def solution(mesh):
    placed = (P("aux", "pair", None, None), P("pair", None), P("pair"), P(), P(), P(), P(), P())
    return jax.shard_map(
        per_device,
        mesh=mesh,
        in_specs=placed,
        out_specs=(P("aux"), P("pair", None)),
        check_vma=False,
    )
```

```python
import functools

import jax
import jax.numpy as jnp
from jax import lax
from jax.experimental import pallas as pl
from jax.experimental.pallas import tpu as pltpu
from jax.sharding import PartitionSpec as P

F32, BF16, I32 = jnp.float32, jnp.bfloat16, jnp.int32
MESH = pl.DeviceIdType.MESH
NX, NY, NZ, NC = 4, 4, 8, 2
NT = (((1,), (1,)), ((), ()))
DMA = pltpu.SemaphoreType.DMA


def dot(a, b, dims=(((1,), (0,)), ((), ()))):
    return lax.dot_general(a, b, dims, preferred_element_type=F32)


def onehot(mask):
    return jnp.where(mask, 1.0, 0.0).astype(BF16)


def iota(shape, axis):
    return lax.broadcasted_iota(I32, shape, axis)


def kernel(
    ids, count, pick_s, eocc,
    ints_hbm, vir_hbm, occ, pick_v, evir,
    out_d, out_e,
    ints, vir, lhs, half, vir_t, vt, meta, meta_in,
    far, near, relay, part,
    cbuf, core_in, x_out, x_in, zsum, z_out, z_in, call,
    dblk, d_in, dy, zr_in, fin,
    ints_sem, vir_sem, meta_ss, meta_rs, far_ss, far_rs, near_ss, near_rs, part_ss, part_rs,
    core_ss, core_rs, x_ss, x_rs, z_ss, z_rs, ag_ss, ag_rs, y_ss, y_rs,
    zr_ss, zr_rs, zg_ss, zg_rs, f_ss, f_rs,
):
    a = lax.axis_index("aux")
    p = lax.axis_index("pair")
    c = lax.rem(a, NC)
    z = lax.rem(lax.div(a, NC), NZ)
    x = lax.div(a, NC * NZ)

    def dev(px, py, pz, pc):
        return {"aux": (px * NZ + pz) * NC + pc, "pair": py}

    def remote(src, dst, ss, rs, to):
        return pltpu.make_async_remote_copy(
            src_ref=src, dst_ref=dst, send_sem=ss, recv_sem=rs, device_id=to, device_id_type=MESH
        )

    def ypeer(step):
        return dev(x, lax.rem(p + step + NY, NY), z, c)

    loads = [pltpu.make_async_copy(ints_hbm.at[s], ints.at[s], ints_sem.at[s]) for s in range(4)]
    for load in loads:
        load.start()
    vir_load = pltpu.make_async_copy(vir_hbm, vir, vir_sem)
    vir_load.start()

    barrier = pltpu.get_barrier_semaphore()

    def greet(to):
        pl.semaphore_signal(barrier, inc=1, device_id=to, device_id_type=MESH)

    for step in range(1, NY):
        greet(ypeer(step))

    def greet_xc(o, carry):
        s = lax.rem(x * NC + c + o, NX * NC)
        greet(dev(lax.div(s, NC), p, z, lax.rem(s, NC)))
        return carry

    lax.fori_loop(1, NX * NC, greet_xc, 0)

    def greet_z(o, carry):
        pz = lax.rem(z + o, NZ)
        greet(dev(x, p, pz, c))
        return carry

    lax.fori_loop(1, NZ, greet_z, 0)

    lane = iota((8, 256), 1)
    slot = lax.shift_right_logical(lane, 6)
    mine = jnp.full((8, 256), ids[0, 0], I32)
    for k in range(1, 4):
        mine = jnp.where(slot == k, ids[0, k], mine)
    meta[...] = jnp.where(slot < count[0], mine * 64 + (lane & 63), -1)

    pick_t = onehot(iota((512, 64), 0) == pick_v[:, 0:64])
    rows = jnp.concatenate([occ[ids[1, s]] for s in range(4)], axis=0)
    chosen = dot(rows, pick_t).astype(BF16)
    r = iota((512, 64), 0)
    orbital = (lax.shift_right_logical(r, 3) & 1) * 32 + (lax.shift_right_logical(r, 4) & 3) * 8
    orbital = orbital + lax.shift_right_logical(r, 6)
    spread = onehot(iota((512, 64), 1) == orbital)
    same = (iota((512, 512), 0) & 7) == lax.shift_right_logical(iota((512, 512), 1), 6)
    for s in range(4):
        tiled = jnp.concatenate([chosen[s * 64 : s * 64 + 64]] * 8, axis=0)
        lhs[s] = jnp.where(same, dot(spread, tiled, NT), 0.0).astype(BF16)

    pl.semaphore_wait(barrier, 3 + 7 + 7)

    metas = [
        remote(meta, meta_in.at[0], meta_ss.at[0], meta_rs.at[0], ypeer(-1)),
        remote(meta, meta_in.at[1], meta_ss.at[1], meta_rs.at[1], ypeer(1)),
    ]
    for m in metas:
        m.start()
    for load in loads:
        load.wait()

    def way(j):
        return 1 - 2 * (j & 1)

    def far_copy(j):
        t = lax.rem(p + 2, NY)
        return remote(half.at[pl.ds(j * 8 + t * 2, 2)], far.at[j], far_ss.at[j], far_rs.at[j], ypeer(way(j)))

    def near_copy(j):
        t = lax.rem(p - way(j) + NY, NY)
        return remote(half.at[pl.ds(j * 8 + t * 2, 2)], near.at[j], near_ss.at[j], near_rs.at[j], ypeer(-way(j)))

    def part_copy(j):
        return remote(relay.at[j], part.at[j], part_ss.at[j], part_rs.at[j], ypeer(way(j)))

    def half_rows(low, n):
        def one_slot(s, carry):
            rows = lhs[s, low * 8 : (low + n) * 8, :]
            for h in range(4):
                u = dot(rows, ints[s, 2 * h]).reshape(n, 8, 256)
                v = dot(rows, ints[s, 2 * h + 1]).reshape(n, 8, 256)
                block = jnp.concatenate([u, v], axis=1).astype(BF16)
                half[low : low + n, pl.ds(pl.multiple_of(s * 64 + h * 16, 16), 16), :] = block
            return carry

        lax.fori_loop(0, 4, one_slot, 0)
        for j in range(low // 8, (low + n) // 8):
            far_copy(j).start()

    half_rows(0, 16)
    half_rows(16, 48)

    vir_load.wait()
    vir_t[...] = vir[...].astype(F32).T.astype(BF16)
    row = iota((1024, 256), 0)
    vt[0] = dot(vir_t[...], onehot(row == meta[0:1, :])).astype(BF16)
    for g in range(2):
        metas[g].wait_recv()
        vt[1 + g] = dot(vir_t[...], onehot(row == meta_in[g, 0:1, :])).astype(BF16)

    def do_relay(j):
        far_copy(j).wait_recv()
        t = lax.rem(p + way(j) + NY, NY)
        for gh in range(2):
            total = dot(vt[2 - (j & 1)], far[j, gh]) + dot(vt[0], half[j * 8 + t * 2 + gh])
            relay[j, gh] = total.astype(BF16)
        part_copy(j).start()
        near_copy(j).start()

    def core_copy(j):
        return remote(cbuf.at[j, 1 - c], core_in.at[j], core_ss.at[j], core_rs.at[j], dev(x, p, z, 1 - c))

    def x_copy(j, o):
        q = lax.rem(x + o, NX)
        return remote(
            x_out.at[j, q], x_in.at[j, o - 1], x_ss.at[j, o - 1], x_rs.at[j, o - 1], dev(q, p, z, c)
        )

    def z_copy(j, o):
        return remote(z_out.at[j], z_in.at[o - 1], z_ss.at[j], z_rs.at[o - 1], dev(x, p, j, c))

    def do_target(j):
        near_copy(j).wait_recv()
        part_copy(j).wait_recv()
        fitted = []
        for gh in range(2):
            total = part[j, gh].astype(F32) + dot(vt[1 + (j & 1)], near[j, gh])
            total = total + dot(vt[0], half[j * 8 + p * 2 + gh])
            fitted.append(total.astype(BF16))
        block = dot(fitted[0], fitted[1], NT)
        for q in range(4):
            for pc in range(2):
                lo = q * 96 + pc * 48
                cbuf[j, pc, q] = block[lo : lo + 48]
        core_copy(j).start()

    def do_core(j):
        core_copy(j).wait_recv()
        both = core_in[j] + cbuf[j, c]
        core_in[j] = both
        x_out[j] = both.astype(BF16)
        for o in range(1, NX):
            x_copy(j, o).start()

    def do_x(j):
        total = core_in[j, x]
        for o in range(1, NX):
            x_copy(j, o).wait_recv()
            total = total + x_in[j, o - 1].astype(F32)
        zsum[j] = total
        z_out[j] = total.astype(BF16)

        @pl.when(z != j)
        def _():
            z_copy(j, lax.rem(z - j + NZ, NZ)).start()

    def step(n, carry):
        @pl.when(n < 8)
        def _():
            do_relay(n)

        @pl.when(n > 3)
        def _():
            do_core(n - 4)
            do_x(n - 4)

        @pl.when(n > 2)
        def _():
            do_target(n - 3)

        return carry

    lax.fori_loop(0, 11, step, 0)
    do_core(7)
    do_x(7)

    total = zsum[z]
    for o in range(1, NZ):
        z_copy(z, o).wait_recv()
        total = total + z_in[o - 1].astype(F32)
    slab = x * NC + c
    call[slab] = total.astype(BF16)

    def ag_copy(o, src):
        s = lax.rem(slab + o, NX * NC)
        to = dev(lax.div(s, NC), p, z, lax.rem(s, NC))
        return remote(call.at[src], call.at[src], ag_ss.at[o - 1], ag_rs.at[src], to)

    for o in range(1, NX * NC):
        ag_copy(o, slab).start()
    for o in range(1, NX * NC):
        ag_copy(o, lax.rem(slab + o, NX * NC)).wait_recv()

    k = p * NZ + z
    level = eocc[pick_s[k]] + eocc[pick_s[k + 32]]
    block = call[...].astype(F32).reshape(384, 384)
    block_t = block.T
    across = jnp.broadcast_to(evir[...].reshape(1, 384), (384, 384))
    denom = level - across.T - across
    amplitude = block / denom
    energy = jnp.sum(amplitude * (2.0 * block - block_t))
    amplitude_t = block_t / denom

    high = functools.partial(
        lax.dot_general, precision=lax.Precision.HIGHEST, preferred_element_type=F32
    )
    rank = iota((64, 384), 0) & 15
    wanted = lax.shift_right_logical(iota((64, 384), 0), 4) * 96 + slab * 12 + rank
    chosen = jnp.where((iota((64, 384), 1) == wanted) & (rank < 12), 1.0, 0.0)
    plain = (((1,), (0,)), ((), ()))
    share = high(high(chosen, 2.0 * amplitude - amplitude_t, plain), amplitude_t, plain)
    share = share + high(high(chosen, 2.0 * amplitude_t - amplitude, plain), amplitude, plain)
    share = share + jnp.where((iota((64, 384), 1) == k) & (rank == 12), energy, 0.0)
    for y in range(4):
        dblk[y] = share[y * 16 : y * 16 + 16]

    def y_copy(o):
        y = lax.rem(p + o, NY)
        return remote(dblk.at[y], d_in.at[o - 1], y_ss.at[o - 1], y_rs.at[o - 1], dev(x, y, z, c))

    for o in range(1, NY):
        y_copy(o).start()
    total = dblk[p]
    for o in range(1, NY):
        y_copy(o).wait_recv()
        total = total + d_in[o - 1]
    dy[...] = total.reshape(8, 2, 384)

    def zr_copy(o):
        pz = lax.rem(z + o, NZ)
        return remote(dy.at[pz], zr_in.at[o - 1], zr_ss.at[o - 1], zr_rs.at[o - 1], dev(x, p, pz, c))

    def zg_copy(o, src):
        pz = lax.rem(z + o, NZ)
        return remote(fin.at[slab, src], fin.at[slab, src], zg_ss.at[o - 1], zg_rs.at[src], dev(x, p, pz, c))

    def f_copy(o, src):
        to = lax.rem(slab + o, NX * NC)
        return remote(fin.at[src], fin.at[src], f_ss.at[o - 1], f_rs.at[src], dev(lax.div(to, NC), p, z, lax.rem(to, NC)))

    for o in range(1, NZ):
        zr_copy(o).start()
    total = dy[z]
    for o in range(1, NZ):
        zr_copy(o).wait_recv()
        total = total + zr_in[o - 1]
    fin[slab, z] = total
    for o in range(1, NZ):
        zg_copy(o, z).start()
    for o in range(1, NZ):
        zg_copy(o, lax.rem(z + o, NZ)).wait_recv()
    for o in range(1, NX * NC):
        f_copy(o, slab).start()
    for o in range(1, NX * NC):
        f_copy(o, lax.rem(slab + o, NX * NC)).wait_recv()

    out_d[...] = fin[:, 0:6].reshape(96, 384)
    out_e[0] = jnp.sum(jnp.where(iota((1, 384), 1) == lax.rem(a, 32), fin[0, 6][0:1, :], 0.0))

    for m in metas:
        m.wait_send()

    def sent(j, carry):
        far_copy(j).wait_send()
        near_copy(j).wait_send()
        part_copy(j).wait_send()
        core_copy(j).wait_send()
        for o in range(1, NX):
            x_copy(j, o).wait_send()

        @pl.when(z != j)
        def _():
            z_copy(j, 1).wait_send()

        return carry

    lax.fori_loop(0, 8, sent, 0)
    for o in range(1, NX * NC):
        ag_copy(o, slab).wait_send()
        f_copy(o, slab).wait_send()
    for o in range(1, NY):
        y_copy(o).wait_send()
    for o in range(1, NZ):
        zr_copy(o).wait_send()
        zg_copy(o, z).wait_send()


def per_device(
    shell_ints, block_ids, block_count, occ_coef, occ_pick, vir_coef, occ_energy, vir_energy
):
    ints = jnp.transpose(shell_ints, (1, 2, 3, 0)).reshape(4, 8, 512, 256)
    smem = pl.BlockSpec(memory_space=pltpu.SMEM)
    vmem = pl.BlockSpec(memory_space=pltpu.VMEM)
    density, energy = pl.pallas_call(
        kernel,
        out_shape=(jax.ShapeDtypeStruct((96, 384), F32), jax.ShapeDtypeStruct((1,), F32)),
        in_specs=[smem] * 4 + [pl.BlockSpec(memory_space=pl.ANY)] * 2 + [vmem] * 3,
        out_specs=(vmem, smem),
        scratch_shapes=[
            pltpu.VMEM((4, 8, 512, 256), BF16),
            pltpu.VMEM((1024, 384), BF16),
            pltpu.VMEM((4, 512, 512), BF16),
            pltpu.VMEM((64, 256, 256), BF16),
            pltpu.VMEM((384, 1024), BF16),
            pltpu.VMEM((3, 384, 256), BF16),
            pltpu.VMEM((8, 256), I32),
            pltpu.VMEM((2, 8, 256), I32),
            pltpu.VMEM((8, 2, 256, 256), BF16),
            pltpu.VMEM((8, 2, 256, 256), BF16),
            pltpu.VMEM((8, 2, 384, 256), BF16),
            pltpu.VMEM((8, 2, 384, 256), BF16),
            pltpu.VMEM((8, 2, 4, 48, 384), F32),
            pltpu.VMEM((8, 4, 48, 384), F32),
            pltpu.VMEM((8, 4, 48, 384), BF16),
            pltpu.VMEM((8, 3, 48, 384), BF16),
            pltpu.VMEM((8, 48, 384), F32),
            pltpu.VMEM((8, 48, 384), BF16),
            pltpu.VMEM((7, 48, 384), BF16),
            pltpu.VMEM((8, 48, 384), BF16),
            pltpu.VMEM((4, 16, 384), F32),
            pltpu.VMEM((3, 16, 384), F32),
            pltpu.VMEM((8, 2, 384), F32),
            pltpu.VMEM((7, 2, 384), F32),
            pltpu.VMEM((8, 8, 2, 384), F32),
            DMA((4,)), DMA,
            DMA((2,)), DMA((2,)),
            DMA((8,)), DMA((8,)),
            DMA((8,)), DMA((8,)),
            DMA((8,)), DMA((8,)),
            DMA((8,)), DMA((8,)),
            DMA((8, 3)), DMA((8, 3)),
            DMA((8,)), DMA((7,)),
            DMA((7,)), DMA((8,)),
            DMA((3,)), DMA((3,)),
            DMA((7,)), DMA((7,)),
            DMA((7,)), DMA((8,)),
            DMA((7,)), DMA((8,)),
        ],
        compiler_params=pltpu.CompilerParams(
            collective_id=0, has_side_effects=True, vmem_limit_bytes=56 << 20
        ),
    )(
        block_ids.T, block_count, occ_pick, occ_energy,
        ints, vir_coef.reshape(1024, 384), occ_coef, occ_pick.reshape(1, 512), vir_energy,
    )
    return (energy, density)


def solution(mesh):
    placed = (P("aux", "pair", None, None), P("pair", None), P("pair"), P(), P(), P(), P(), P())
    return jax.shard_map(
        per_device,
        mesh=mesh,
        in_specs=placed,
        out_specs=(P("aux"), P("pair", None)),
        check_vma=False,
    )
```

```python
import functools

import jax
import jax.numpy as jnp
from jax import lax
from jax.experimental import pallas as pl
from jax.experimental.pallas import tpu as pltpu
from jax.sharding import PartitionSpec as P

F32, BF16, I32 = jnp.float32, jnp.bfloat16, jnp.int32
MESH = pl.DeviceIdType.MESH
NX, NY, NZ, NC = 4, 4, 8, 2
NT = (((1,), (1,)), ((), ()))
DMA = pltpu.SemaphoreType.DMA


def dot(a, b, dims=(((1,), (0,)), ((), ()))):
    return lax.dot_general(a, b, dims, preferred_element_type=F32)


def onehot(mask):
    return jnp.where(mask, 1.0, 0.0).astype(BF16)


def iota(shape, axis):
    return lax.broadcasted_iota(I32, shape, axis)


def kernel(
    ids, count,
    ints_hbm, vir_hbm, occ_hbm, pick_hbm, eocc_hbm, evir_hbm,
    out_d, out_e,
    ints, vir, occ, pick, eocc, evir, lhs, half, vir_t, vt, meta, meta_in,
    far, near, relay, part,
    cbuf, core_in, x_out, x_in, zsum, z_out, z_in, call,
    dblk, d_in, line_in, fin,
    load_sem, met,
    meta_ss, meta_rs, far_ss, far_rs, near_ss, near_rs, part_ss, part_rs,
    core_ss, core_rs, x_ss, x_rs, z_ss, z_rs, ag_ss, ag_rs, y_ss, y_rs,
    line_ss, line_rs, f_ss, f_rs,
):
    a = lax.axis_index("aux")
    p = lax.axis_index("pair")
    c = lax.rem(a, NC)
    z = lax.rem(lax.div(a, NC), NZ)
    x = lax.div(a, NC * NZ)

    def dev(px, py, pz, pc):
        return {"aux": (px * NZ + pz) * NC + pc, "pair": py}

    def remote(src, dst, ss, rs, to):
        return pltpu.make_async_remote_copy(
            src_ref=src, dst_ref=dst, send_sem=ss, recv_sem=rs, device_id=to, device_id_type=MESH
        )

    def ypeer(step):
        return dev(x, lax.rem(p + step + NY, NY), z, c)

    barrier = pltpu.get_barrier_semaphore()
    beside = [
        dev(x, p, z, 1 - c),
        dev(lax.rem(x + 1, NX), p, z, c),
        dev(lax.rem(x + NX - 1, NX), p, z, c),
        dev(x, p, lax.rem(z + 1, NZ), c),
        dev(x, p, lax.rem(z + NZ - 1, NZ), c),
    ]
    for to in [ypeer(1), ypeer(-1)] + beside:
        pl.semaphore_signal(barrier, inc=1, device_id=to, device_id_type=MESH)

    small = [
        pltpu.make_async_copy(src, dst, load_sem.at[i])
        for i, (src, dst) in enumerate(
            ((pick_hbm, pick), (occ_hbm, occ), (eocc_hbm, eocc), (evir_hbm, evir), (vir_hbm, vir))
        )
    ]
    loads = [pltpu.make_async_copy(ints_hbm.at[s], ints.at[s], load_sem.at[5 + s]) for s in range(4)]
    for load in small[:2] + loads + small[2:]:
        load.start()

    lane = iota((8, 256), 1)
    slot = lax.shift_right_logical(lane, 6)
    mine = jnp.full((8, 256), ids[0, 0], I32)
    for k in range(1, 4):
        mine = jnp.where(slot == k, ids[0, k], mine)
    meta[...] = jnp.where(slot < count[0], mine * 64 + (lane & 63), -1)

    small[0].wait()
    small[1].wait()
    pick_t = onehot(iota((512, 64), 0) == pick[:, 0:64])
    rows = jnp.concatenate([occ[ids[1, s]] for s in range(4)], axis=0)
    chosen = dot(rows, pick_t).astype(BF16)
    r = iota((512, 64), 0)
    orbital = (lax.shift_right_logical(r, 3) & 1) * 32 + (lax.shift_right_logical(r, 4) & 3) * 8
    orbital = orbital + lax.shift_right_logical(r, 6)
    spread = onehot(iota((512, 64), 1) == orbital)
    same = (iota((512, 512), 0) & 7) == lax.shift_right_logical(iota((512, 512), 1), 6)
    for s in range(4):
        tiled = jnp.concatenate([chosen[s * 64 : s * 64 + 64]] * 8, axis=0)
        lhs[s] = jnp.where(same, dot(spread, tiled, NT), 0.0).astype(BF16)

    pl.semaphore_wait(barrier, 7)

    metas = [
        remote(meta, meta_in.at[0], meta_ss.at[0], meta_rs.at[0], ypeer(-1)),
        remote(meta, meta_in.at[1], meta_ss.at[1], meta_rs.at[1], ypeer(1)),
    ]
    for m in metas:
        m.start()
    for load in loads:
        load.wait()

    def way(j):
        return 1 - 2 * (j & 1)

    def far_copy(j):
        t = lax.rem(p + 2, NY)
        return remote(half.at[pl.ds(j * 8 + t * 2, 2)], far.at[j], far_ss.at[j], far_rs.at[j], ypeer(way(j)))

    def near_copy(j):
        t = lax.rem(p - way(j) + NY, NY)
        return remote(half.at[pl.ds(j * 8 + t * 2, 2)], near.at[j], near_ss.at[j], near_rs.at[j], ypeer(-way(j)))

    def part_copy(j):
        return remote(relay.at[j], part.at[j], part_ss.at[j], part_rs.at[j], ypeer(way(j)))

    def half_rows(low, n):
        def one_slot(s, carry):
            rows = lhs[s, low * 8 : (low + n) * 8, :]
            for h in range(4):
                u = dot(rows, ints[s, 2 * h]).reshape(n, 8, 256)
                v = dot(rows, ints[s, 2 * h + 1]).reshape(n, 8, 256)
                block = jnp.concatenate([u, v], axis=1).astype(BF16)
                half[low : low + n, pl.ds(pl.multiple_of(s * 64 + h * 16, 16), 16), :] = block
            return carry

        lax.fori_loop(0, 4, one_slot, 0)
        for j in range(low // 8, (low + n) // 8):
            far_copy(j).start()

    half_rows(0, 16)
    half_rows(16, 48)

    for r in range(3):
        for to in beside:
            pl.semaphore_signal(met.at[r], inc=1, device_id=to, device_id_type=MESH)
        pl.semaphore_wait(met.at[r], 5)

    for load in small[2:]:
        load.wait()
    vir_t[...] = vir[...].astype(F32).T.astype(BF16)
    row = iota((1024, 256), 0)
    vt[0] = dot(vir_t[...], onehot(row == meta[0:1, :])).astype(BF16)
    for g in range(2):
        metas[g].wait_recv()
        vt[1 + g] = dot(vir_t[...], onehot(row == meta_in[g, 0:1, :])).astype(BF16)

    def do_relay(j):
        far_copy(j).wait_recv()
        t = lax.rem(p + way(j) + NY, NY)
        for gh in range(2):
            total = dot(vt[2 - (j & 1)], far[j, gh]) + dot(vt[0], half[j * 8 + t * 2 + gh])
            relay[j, gh] = total.astype(BF16)
        part_copy(j).start()
        near_copy(j).start()

    def core_copy(j):
        return remote(cbuf.at[j, 1 - c], core_in.at[j], core_ss.at[j], core_rs.at[j], dev(x, p, z, 1 - c))

    def x_copy(j, o):
        q = lax.rem(x + o, NX)
        return remote(
            x_out.at[j, q], x_in.at[j, o - 1], x_ss.at[j, o - 1], x_rs.at[j, o - 1], dev(q, p, z, c)
        )

    def z_copy(j, o):
        return remote(z_out.at[j], z_in.at[o - 1], z_ss.at[j], z_rs.at[o - 1], dev(x, p, j, c))

    def do_target(j):
        near_copy(j).wait_recv()
        part_copy(j).wait_recv()
        fitted = []
        for gh in range(2):
            total = part[j, gh].astype(F32) + dot(vt[1 + (j & 1)], near[j, gh])
            total = total + dot(vt[0], half[j * 8 + p * 2 + gh])
            fitted.append(total.astype(BF16))
        block = dot(fitted[0], fitted[1], NT)
        for q in range(4):
            for pc in range(2):
                lo = q * 96 + pc * 48
                cbuf[j, pc, q] = block[lo : lo + 48]
        core_copy(j).start()

    def do_core(j):
        core_copy(j).wait_recv()
        both = core_in[j] + cbuf[j, c]
        core_in[j] = both
        x_out[j] = both.astype(BF16)
        for o in range(1, NX):
            x_copy(j, o).start()

    def do_x(j):
        total = core_in[j, x]
        for o in range(1, NX):
            x_copy(j, o).wait_recv()
            total = total + x_in[j, o - 1].astype(F32)
        zsum[j] = total
        z_out[j] = total.astype(BF16)

        @pl.when(z != j)
        def _():
            z_copy(j, lax.rem(z - j + NZ, NZ)).start()

    def step(n, carry):
        @pl.when(n < 8)
        def _():
            do_relay(n)

        @pl.when(n > 3)
        def _():
            do_core(n - 4)
            do_x(n - 4)

        @pl.when(n > 2)
        def _():
            do_target(n - 3)

        return carry

    lax.fori_loop(0, 11, step, 0)
    do_core(7)
    do_x(7)

    total = zsum[z]
    for o in range(1, NZ):
        z_copy(z, o).wait_recv()
        total = total + z_in[o - 1].astype(F32)
    slab = x * NC + c
    call[slab] = total.astype(BF16)

    def ag_copy(o, src):
        s = lax.rem(slab + o, NX * NC)
        to = dev(lax.div(s, NC), p, z, lax.rem(s, NC))
        return remote(call.at[src], call.at[src], ag_ss.at[o - 1], ag_rs.at[src], to)

    for o in range(1, NX * NC):
        ag_copy(o, slab).start()
    for o in range(1, NX * NC):
        ag_copy(o, lax.rem(slab + o, NX * NC)).wait_recv()

    k = p * NZ + z
    where = iota((1, 512), 1)
    level = 0.0
    for g in (k, k + 32):
        orbital = jnp.sum(jnp.where(where == g, pick[...], 0))
        level = level + jnp.sum(jnp.where(where == orbital, eocc[...], 0.0))
    block = call[...].astype(F32).reshape(384, 384)
    block_t = block.T
    across = jnp.broadcast_to(evir[...].reshape(1, 384), (384, 384))
    denom = level - across.T - across
    amplitude = block / denom
    energy = jnp.sum(amplitude * (2.0 * block - block_t))
    amplitude_t = block_t / denom

    high = functools.partial(
        lax.dot_general, precision=lax.Precision.HIGHEST, preferred_element_type=F32
    )
    rank = iota((64, 384), 0) & 15
    wanted = lax.shift_right_logical(iota((64, 384), 0), 4) * 96 + slab * 12 + rank
    chosen = jnp.where((iota((64, 384), 1) == wanted) & (rank < 12), 1.0, 0.0)
    plain = (((1,), (0,)), ((), ()))
    share = high(high(chosen, 2.0 * amplitude - amplitude_t, plain), amplitude_t, plain)
    share = share + high(high(chosen, 2.0 * amplitude_t - amplitude, plain), amplitude, plain)
    share = share + jnp.where((iota((64, 384), 1) == k) & ((rank == 12) | (rank == 13)), energy, 0.0)
    for y in range(4):
        dblk[y] = share[y * 16 : y * 16 + 16]

    def y_copy(o):
        y = lax.rem(p + o, NY)
        return remote(dblk.at[y], d_in.at[o - 1], y_ss.at[o - 1], y_rs.at[o - 1], dev(x, y, z, c))

    for o in range(1, NY):
        y_copy(o).start()
    total = dblk[p]
    for o in range(1, NY):
        y_copy(o).wait_recv()
        total = total + d_in[o - 1]
    rest = total - total.astype(BF16).astype(F32)
    line_in[z] = jnp.where(iota((16, 384), 0) == 13, rest, total).astype(BF16)

    def line_copy(o, src):
        pz = lax.rem(z + o, NZ)
        return remote(line_in.at[src], line_in.at[src], line_ss.at[o - 1], line_rs.at[src], dev(x, p, pz, c))

    def f_copy(o, src):
        to = lax.rem(slab + o, NX * NC)
        return remote(fin.at[src], fin.at[src], f_ss.at[o - 1], f_rs.at[src], dev(lax.div(to, NC), p, z, lax.rem(to, NC)))

    for o in (4, 3, 5, 2, 6, 1, 7):
        line_copy(o, z).start()
    for o in range(1, NZ):
        line_copy(o, lax.rem(z + o, NZ)).wait_recv()
    total = line_in[0].astype(F32)
    for o in range(1, NZ):
        total = total + line_in[o].astype(F32)
    fin[slab] = total
    for o in (4, 5, 3, 2, 6, 1, 7):
        f_copy(o, slab).start()
    for o in range(1, NX * NC):
        f_copy(o, lax.rem(slab + o, NX * NC)).wait_recv()

    for s in range(NX * NC):
        out_d[s * 12 : s * 12 + 12, :] = fin[s, 0:12]
    energies = fin[0, 12:13] + fin[0, 13:14]
    out_e[0] = jnp.sum(jnp.where(iota((1, 384), 1) == lax.rem(a, 32), energies, 0.0))

    for m in metas:
        m.wait_send()

    def sent(j, carry):
        far_copy(j).wait_send()
        near_copy(j).wait_send()
        part_copy(j).wait_send()
        core_copy(j).wait_send()
        for o in range(1, NX):
            x_copy(j, o).wait_send()

        @pl.when(z != j)
        def _():
            z_copy(j, 1).wait_send()

        return carry

    lax.fori_loop(0, 8, sent, 0)
    for o in range(1, NX * NC):
        ag_copy(o, slab).wait_send()
        f_copy(o, slab).wait_send()
    for o in range(1, NY):
        y_copy(o).wait_send()
    for o in range(1, NZ):
        line_copy(o, z).wait_send()


def per_device(
    shell_ints, block_ids, block_count, occ_coef, occ_pick, vir_coef, occ_energy, vir_energy
):
    ints = jnp.transpose(shell_ints, (1, 2, 3, 0)).reshape(4, 8, 512, 256)
    smem = pl.BlockSpec(memory_space=pltpu.SMEM)
    vmem = pl.BlockSpec(memory_space=pltpu.VMEM)
    density, energy = pl.pallas_call(
        kernel,
        out_shape=(jax.ShapeDtypeStruct((96, 384), F32), jax.ShapeDtypeStruct((1,), F32)),
        in_specs=[smem] * 2 + [pl.BlockSpec(memory_space=pl.ANY)] * 6,
        out_specs=(vmem, smem),
        scratch_shapes=[
            pltpu.VMEM((4, 8, 512, 256), BF16),
            pltpu.VMEM((1024, 384), BF16),
            pltpu.VMEM((16, 64, 512), BF16),
            pltpu.VMEM((1, 512), I32),
            pltpu.VMEM((1, 512), F32),
            pltpu.VMEM((384,), F32),
            pltpu.VMEM((4, 512, 512), BF16),
            pltpu.VMEM((64, 256, 256), BF16),
            pltpu.VMEM((384, 1024), BF16),
            pltpu.VMEM((3, 384, 256), BF16),
            pltpu.VMEM((8, 256), I32),
            pltpu.VMEM((2, 8, 256), I32),
            pltpu.VMEM((8, 2, 256, 256), BF16),
            pltpu.VMEM((8, 2, 256, 256), BF16),
            pltpu.VMEM((8, 2, 384, 256), BF16),
            pltpu.VMEM((8, 2, 384, 256), BF16),
            pltpu.VMEM((8, 2, 4, 48, 384), F32),
            pltpu.VMEM((8, 4, 48, 384), F32),
            pltpu.VMEM((8, 4, 48, 384), BF16),
            pltpu.VMEM((8, 3, 48, 384), BF16),
            pltpu.VMEM((8, 48, 384), F32),
            pltpu.VMEM((8, 48, 384), BF16),
            pltpu.VMEM((7, 48, 384), BF16),
            pltpu.VMEM((8, 48, 384), BF16),
            pltpu.VMEM((4, 16, 384), F32),
            pltpu.VMEM((3, 16, 384), F32),
            pltpu.VMEM((8, 16, 384), BF16),
            pltpu.VMEM((8, 16, 384), F32),
            DMA((9,)), pltpu.SemaphoreType.REGULAR((3,)),
            DMA((2,)), DMA((2,)),
            DMA((8,)), DMA((8,)),
            DMA((8,)), DMA((8,)),
            DMA((8,)), DMA((8,)),
            DMA((8,)), DMA((8,)),
            DMA((8, 3)), DMA((8, 3)),
            DMA((8,)), DMA((7,)),
            DMA((7,)), DMA((8,)),
            DMA((3,)), DMA((3,)),
            DMA((7,)), DMA((8,)),
            DMA((7,)), DMA((8,)),
        ],
        compiler_params=pltpu.CompilerParams(
            collective_id=0, has_side_effects=True, vmem_limit_bytes=56 << 20
        ),
    )(
        block_ids.T, block_count,
        ints, vir_coef.reshape(1024, 384), occ_coef, occ_pick.reshape(1, 512), occ_energy.reshape(1, 512), vir_energy,
    )
    return (energy, density)


def solution(mesh):
    placed = (P("aux", "pair", None, None), P("pair", None), P("pair"), P(), P(), P(), P(), P())
    return jax.shard_map(
        per_device,
        mesh=mesh,
        in_specs=placed,
        out_specs=(P("aux"), P("pair", None)),
        check_vma=False,
    )
```

```python
import functools

import jax
import jax.numpy as jnp
from jax import lax
from jax.experimental import pallas as pl
from jax.experimental.pallas import tpu as pltpu
from jax.sharding import PartitionSpec as P

F32, BF16, I32 = jnp.float32, jnp.bfloat16, jnp.int32
MESH = pl.DeviceIdType.MESH
NX, NY, NZ, NC = 4, 4, 8, 2
NT = (((1,), (1,)), ((), ()))
DMA = pltpu.SemaphoreType.DMA


def dot(a, b, dims=(((1,), (0,)), ((), ()))):
    return lax.dot_general(a, b, dims, preferred_element_type=F32)


def onehot(mask):
    return jnp.where(mask, 1.0, 0.0).astype(BF16)


def iota(shape, axis):
    return lax.broadcasted_iota(I32, shape, axis)


def kernel(
    ids, count,
    ints_hbm, vir_hbm, occ_hbm, pick_hbm, eocc_hbm, evir_hbm,
    out,
    ints, vir, occ, pick, eocc, evir, lhs, half, vir_t, vt, meta, meta_in,
    far, near, relay, part,
    cbuf, core_in, x_out, x_in, zsum, z_out, z_in, call, weight, mix,
    dblk, d_in, line_in, fin,
    load_sem, met,
    meta_ss, meta_rs, far_ss, far_rs, near_ss, near_rs, part_ss, part_rs,
    core_ss, core_rs, x_ss, x_rs, z_ss, z_rs, ag_ss, ag_rs, y_ss, y_rs,
    line_ss, line_rs, f_ss, f_rs,
):
    a = lax.axis_index("aux")
    p = lax.axis_index("pair")
    c = lax.rem(a, NC)
    z = lax.rem(lax.div(a, NC), NZ)
    x = lax.div(a, NC * NZ)

    def dev(px, py, pz, pc):
        return {"aux": (px * NZ + pz) * NC + pc, "pair": py}

    def remote(src, dst, ss, rs, to):
        return pltpu.make_async_remote_copy(
            src_ref=src, dst_ref=dst, send_sem=ss, recv_sem=rs, device_id=to, device_id_type=MESH
        )

    def ypeer(step):
        return dev(x, lax.rem(p + step + NY, NY), z, c)

    barrier = pltpu.get_barrier_semaphore()
    beside = [
        dev(x, p, z, 1 - c),
        dev(lax.rem(x + 1, NX), p, z, c),
        dev(lax.rem(x + NX - 1, NX), p, z, c),
        dev(x, p, lax.rem(z + 1, NZ), c),
        dev(x, p, lax.rem(z + NZ - 1, NZ), c),
    ]
    for to in [ypeer(1), ypeer(-1)] + beside:
        pl.semaphore_signal(barrier, inc=1, device_id=to, device_id_type=MESH)

    small = [
        pltpu.make_async_copy(src, dst, load_sem.at[i])
        for i, (src, dst) in enumerate(
            ((pick_hbm, pick), (occ_hbm, occ), (eocc_hbm, eocc), (evir_hbm, evir), (vir_hbm, vir))
        )
    ]
    loads = [pltpu.make_async_copy(ints_hbm.at[s], ints.at[s], load_sem.at[5 + s]) for s in range(4)]
    for load in small[:2] + loads + small[2:]:
        load.start()

    lane = iota((8, 256), 1)
    slot = lax.shift_right_logical(lane, 6)
    mine = jnp.full((8, 256), ids[0, 0], I32)
    for k in range(1, 4):
        mine = jnp.where(slot == k, ids[0, k], mine)
    meta[...] = jnp.where(slot < count[0], mine * 64 + (lane & 63), -1)

    small[0].wait()
    small[1].wait()
    pick_t = onehot(iota((512, 64), 0) == pick[:, 0:64])
    rows = jnp.concatenate([occ[ids[1, s]] for s in range(4)], axis=0)
    chosen = dot(rows, pick_t).astype(BF16)
    r = iota((512, 64), 0)
    orbital = (lax.shift_right_logical(r, 3) & 1) * 32 + (lax.shift_right_logical(r, 4) & 3) * 8
    orbital = orbital + lax.shift_right_logical(r, 6)
    spread = onehot(iota((512, 64), 1) == orbital)
    same = (iota((512, 512), 0) & 7) == lax.shift_right_logical(iota((512, 512), 1), 6)
    for s in range(4):
        tiled = jnp.concatenate([chosen[s * 64 : s * 64 + 64]] * 8, axis=0)
        lhs[s] = jnp.where(same, dot(spread, tiled, NT), 0.0).astype(BF16)

    metas = [
        remote(meta, meta_in.at[0], meta_ss.at[0], meta_rs.at[0], ypeer(-1)),
        remote(meta, meta_in.at[1], meta_ss.at[1], meta_rs.at[1], ypeer(1)),
    ]
    for load in loads:
        load.wait()

    def way(j):
        return 1 - 2 * (j & 1)

    def far_copy(j):
        t = lax.rem(p + 2, NY)
        return remote(half.at[pl.ds(j * 8 + t * 2, 2)], far.at[j], far_ss.at[j], far_rs.at[j], ypeer(way(j)))

    def near_copy(j):
        t = lax.rem(p - way(j) + NY, NY)
        return remote(half.at[pl.ds(j * 8 + t * 2, 2)], near.at[j], near_ss.at[j], near_rs.at[j], ypeer(-way(j)))

    def part_copy(j):
        return remote(relay.at[j], part.at[j], part_ss.at[j], part_rs.at[j], ypeer(way(j)))

    def half_rows(low, n):
        def one_slot(s, carry):
            rows = lhs[s, low * 8 : (low + n) * 8, :]
            for h in range(4):
                u = dot(rows, ints[s, 2 * h]).reshape(n, 8, 256)
                v = dot(rows, ints[s, 2 * h + 1]).reshape(n, 8, 256)
                block = jnp.concatenate([u, v], axis=1).astype(BF16)
                half[low : low + n, pl.ds(pl.multiple_of(s * 64 + h * 16, 16), 16), :] = block
            return carry

        lax.fori_loop(0, 4, one_slot, 0)

    half_rows(0, 16)
    pl.semaphore_wait(barrier, 7)
    for m in metas:
        m.start()
    for j in range(2):
        far_copy(j).start()
    half_rows(16, 48)
    for j in range(2, 8):
        far_copy(j).start()

    for r in range(3):
        for to in beside:
            pl.semaphore_signal(met.at[r], inc=1, device_id=to, device_id_type=MESH)
        pl.semaphore_wait(met.at[r], 5)

    for load in small[2:]:
        load.wait()
    vir_t[...] = vir[...].astype(F32).T.astype(BF16)
    row = iota((1024, 256), 0)
    vt[0] = dot(vir_t[...], onehot(row == meta[0:1, :])).astype(BF16)
    for g in range(2):
        metas[g].wait()
        vt[1 + g] = dot(vir_t[...], onehot(row == meta_in[g, 0:1, :])).astype(BF16)

    def do_relay(j):
        far_copy(j).wait_recv()
        t = lax.rem(p + way(j) + NY, NY)
        for gh in range(2):
            total = dot(vt[2 - (j & 1)], far[j, gh]) + dot(vt[0], half[j * 8 + t * 2 + gh])
            relay[j, gh] = total.astype(BF16)
        part_copy(j).start()
        near_copy(j).start()

    def core_copy(j):
        return remote(cbuf.at[j, 1 - c], core_in.at[j], core_ss.at[j], core_rs.at[j], dev(x, p, z, 1 - c))

    def x_copy(j, o):
        q = lax.rem(x + o, NX)
        return remote(
            x_out.at[j, q], x_in.at[j, o - 1], x_ss.at[j, o - 1], x_rs.at[j, o - 1], dev(q, p, z, c)
        )

    def z_copy(j, o):
        return remote(z_out.at[j], z_in.at[o - 1], z_ss.at[j], z_rs.at[o - 1], dev(x, p, j, c))

    def do_target(j):
        near_copy(j).wait_recv()
        part_copy(j).wait_recv()
        fitted = []
        for gh in range(2):
            total = part[j, gh].astype(F32) + dot(vt[1 + (j & 1)], near[j, gh])
            total = total + dot(vt[0], half[j * 8 + p * 2 + gh])
            fitted.append(total.astype(BF16))
        block = dot(fitted[0], fitted[1], NT)
        for q in range(4):
            for pc in range(2):
                lo = q * 96 + pc * 48
                cbuf[j, pc, q] = block[lo : lo + 48]
        core_copy(j).start()

    def do_core(j):
        core_copy(j).wait_recv()
        both = core_in[j] + cbuf[j, c]
        core_in[j] = both
        x_out[j] = both.astype(BF16)
        for o in range(1, NX):
            x_copy(j, o).start()

    def do_x(j):
        total = core_in[j, x]
        for o in range(1, NX):
            x_copy(j, o).wait_recv()
            total = total + x_in[j, o - 1].astype(F32)
        zsum[j] = total
        z_out[j] = total.astype(BF16)

        @pl.when(z != j)
        def _():
            z_copy(j, lax.rem(z - j + NZ, NZ)).start()

    def sent(j):
        far_copy(j).wait_send()
        near_copy(j).wait_send()
        part_copy(j).wait_send()
        core_copy(j).wait_send()
        for o in range(1, NX):
            x_copy(j, o).wait_send()

        @pl.when(z != j)
        def _():
            z_copy(j, 1).wait_send()

    def step(n, carry):
        @pl.when(n < 8)
        def _():
            do_relay(n)

        @pl.when(n > 3)
        def _():
            do_core(n - 4)
            do_x(n - 4)

        @pl.when(n > 2)
        def _():
            do_target(n - 3)

        @pl.when(n > 4)
        def _():
            sent(n - 5)

        return carry

    lax.fori_loop(0, 11, step, 0)
    do_core(7)
    do_x(7)

    total = zsum[z]
    for o in range(1, NZ):
        z_copy(z, o).wait_recv()
        total = total + z_in[o - 1].astype(F32)
    slab = x * NC + c
    call[slab] = total.astype(BF16)

    def ag_copy(o, src):
        s = lax.rem(slab + o, NX * NC)
        to = dev(lax.div(s, NC), p, z, lax.rem(s, NC))
        return remote(call.at[src], call.at[src], ag_ss.at[o - 1], ag_rs.at[src], to)

    for o in range(1, NX * NC):
        ag_copy(o, slab).start()
    k = p * NZ + z
    where = iota((1, 512), 1)
    level = 0.0
    for g in (k, k + 32):
        orbital = jnp.sum(jnp.where(where == g, pick[...], 0))
        level = level + jnp.sum(jnp.where(where == orbital, eocc[...], 0.0))
    across = jnp.broadcast_to(evir[...].reshape(1, 384), (384, 384))
    weight[...] = 1.0 / (level - across.T - across)
    sent(6)
    sent(7)
    for o in range(1, NX * NC):
        ag_copy(o, lax.rem(slab + o, NX * NC)).wait_recv()

    block = call[...].astype(F32).reshape(384, 384)
    block_t = block.T
    amplitude = block * weight[...]
    energy = jnp.sum(amplitude * (2.0 * block - block_t))
    amplitude_t = block_t * weight[...]

    high = functools.partial(
        jnp.dot, precision=lax.Precision.HIGHEST, preferred_element_type=F32
    )
    mix[0] = 2.0 * amplitude - amplitude_t
    mix[1] = 2.0 * amplitude_t - amplitude

    def mine_of(g):
        starts = [pl.multiple_of(y * 96 + x * 24, 8) for y in range(4)]
        return jnp.concatenate([mix[g, pl.ds(start, 24), :] for start in starts], axis=0)

    share = high(mine_of(0), amplitude_t) + high(mine_of(1), amplitude)
    tip = jnp.where(iota((4, 384), 1) == k, energy, 0.0)
    for y in range(4):
        lo = y * 24
        dblk[y, 0:12] = jnp.where(c == 0, share[lo : lo + 12], share[lo + 12 : lo + 24])
        dblk[y, 12:16] = tip

    def y_copy(o):
        y = lax.rem(p + o, NY)
        return remote(dblk.at[y], d_in.at[o - 1], y_ss.at[o - 1], y_rs.at[o - 1], dev(x, y, z, c))

    for o in range(1, NY):
        y_copy(o).start()
    for o in range(1, NX * NC):
        ag_copy(o, slab).wait_send()
    total = dblk[p]
    for o in range(1, NY):
        y_copy(o).wait_recv()
        total = total + d_in[o - 1]
    rest = total - total.astype(BF16).astype(F32)
    line_in[z] = jnp.where(iota((16, 384), 0) == 13, rest, total).astype(BF16)

    def line_copy(o, src):
        pz = lax.rem(z + o, NZ)
        return remote(line_in.at[src], line_in.at[src], line_ss.at[o - 1], line_rs.at[src], dev(x, p, pz, c))

    def f_copy(o, src):
        to = lax.rem(slab + o, NX * NC)
        return remote(fin.at[src], fin.at[src], f_ss.at[o - 1], f_rs.at[src], dev(lax.div(to, NC), p, z, lax.rem(to, NC)))

    for o in (4, 3, 5, 2, 6, 1, 7):
        line_copy(o, z).start()
    for o in range(1, NY):
        y_copy(o).wait_send()
    for o in range(1, NZ):
        line_copy(o, lax.rem(z + o, NZ)).wait_recv()
    total = line_in[0].astype(F32)
    for o in range(1, NZ):
        total = total + line_in[o].astype(F32)
    fin[slab] = total
    for o in (4, 5, 3, 2, 6, 1, 7):
        f_copy(o, slab).start()
    for o in range(1, NZ):
        line_copy(o, z).wait_send()
    for o in range(1, NX * NC):
        f_copy(o, lax.rem(slab + o, NX * NC)).wait_recv()

    out[...] = fin[...]
    for o in range(1, NX * NC):
        f_copy(o, slab).wait_send()


def finish(fin, out_d, out_e):
    for s in range(NX * NC):
        out_d[s * 12 : s * 12 + 12, :] = fin[s, 0:12]
    energies = fin[0, 12:13] + fin[0, 13:14]
    pair = lax.rem(lax.axis_index("aux"), 32)
    out_e[0] = jnp.sum(jnp.where(iota((1, 384), 1) == pair, energies, 0.0))


def per_device(
    shell_ints, block_ids, block_count, occ_coef, occ_pick, vir_coef, occ_energy, vir_energy
):
    ints = jnp.transpose(shell_ints, (1, 2, 3, 0)).reshape(4, 8, 512, 256)
    smem = pl.BlockSpec(memory_space=pltpu.SMEM)
    vmem = pl.BlockSpec(memory_space=pltpu.VMEM)
    rows = pl.pallas_call(
        kernel,
        out_shape=jax.ShapeDtypeStruct((8, 16, 384), F32),
        in_specs=[smem] * 2 + [pl.BlockSpec(memory_space=pl.ANY)] * 6,
        out_specs=vmem,
        scratch_shapes=[
            pltpu.VMEM((4, 8, 512, 256), BF16),
            pltpu.VMEM((1024, 384), BF16),
            pltpu.VMEM((16, 64, 512), BF16),
            pltpu.VMEM((1, 512), I32),
            pltpu.VMEM((1, 512), F32),
            pltpu.VMEM((384,), F32),
            pltpu.VMEM((4, 512, 512), BF16),
            pltpu.VMEM((64, 256, 256), BF16),
            pltpu.VMEM((384, 1024), BF16),
            pltpu.VMEM((3, 384, 256), BF16),
            pltpu.VMEM((8, 256), I32),
            pltpu.VMEM((2, 8, 256), I32),
            pltpu.VMEM((8, 2, 256, 256), BF16),
            pltpu.VMEM((8, 2, 256, 256), BF16),
            pltpu.VMEM((8, 2, 384, 256), BF16),
            pltpu.VMEM((8, 2, 384, 256), BF16),
            pltpu.VMEM((8, 2, 4, 48, 384), F32),
            pltpu.VMEM((8, 4, 48, 384), F32),
            pltpu.VMEM((8, 4, 48, 384), BF16),
            pltpu.VMEM((8, 3, 48, 384), BF16),
            pltpu.VMEM((8, 48, 384), F32),
            pltpu.VMEM((8, 48, 384), BF16),
            pltpu.VMEM((7, 48, 384), BF16),
            pltpu.VMEM((8, 48, 384), BF16),
            pltpu.VMEM((384, 384), F32),
            pltpu.VMEM((2, 384, 384), F32),
            pltpu.VMEM((4, 16, 384), F32),
            pltpu.VMEM((3, 16, 384), F32),
            pltpu.VMEM((8, 16, 384), BF16),
            pltpu.VMEM((8, 16, 384), F32),
            DMA((9,)), pltpu.SemaphoreType.REGULAR((3,)),
            DMA((2,)), DMA((2,)),
            DMA((8,)), DMA((8,)),
            DMA((8,)), DMA((8,)),
            DMA((8,)), DMA((8,)),
            DMA((8,)), DMA((8,)),
            DMA((8, 3)), DMA((8, 3)),
            DMA((8,)), DMA((7,)),
            DMA((7,)), DMA((8,)),
            DMA((3,)), DMA((3,)),
            DMA((7,)), DMA((8,)),
            DMA((7,)), DMA((8,)),
        ],
        compiler_params=pltpu.CompilerParams(
            collective_id=0, has_side_effects=True, vmem_limit_bytes=56 << 20
        ),
    )(
        block_ids.T, block_count,
        ints, vir_coef.reshape(1024, 384), occ_coef, occ_pick.reshape(1, 512), occ_energy.reshape(1, 512), vir_energy,
    )
    density, energy = pl.pallas_call(
        finish,
        out_shape=(jax.ShapeDtypeStruct((96, 384), F32), jax.ShapeDtypeStruct((1,), F32)),
        in_specs=[vmem],
        out_specs=(vmem, smem),
    )(rows)
    return (energy, density)


def solution(mesh):
    placed = (P("aux", "pair", None, None), P("pair", None), P("pair"), P(), P(), P(), P(), P())
    return jax.shard_map(
        per_device,
        mesh=mesh,
        in_specs=placed,
        out_specs=(P("aux"), P("pair", None)),
        check_vma=False,
    )
```
